32 devices in a mesh: expert: 8 (over y, x, core), tensor: 4 (over z).
Axes of the slice: x: 2, y: 2, z: 4, core: 2. Of those that a mesh axis runs over, the one named last changes fastest.
Arguments:
- flow_state: bfloat16 [8192, 2048], P('expert'), may hold values from -6 to 6
- norm_gain: float32 [2048], replicated, may hold values from 0.5 to 1.5
- expert_ids: int32 [8192, 6], P('expert'), may hold values from 0 to 15, all different within a row; in each aligned block of 1024 rows (0 to 1023, 1024 to 2047, ...) at most 512 rows name the same one
- gate_weights: float32 [8192, 6], P('expert'), may hold values from 0.1 to 1
- w_gate: bfloat16 [16, 704, 2048], P('expert', 'tensor'), may hold values from -0.125 to 0.125
- w_up: bfloat16 [16, 704, 2048], P('expert', 'tensor'), may hold values from -0.125 to 0.125
- w_down: bfloat16 [16, 704, 2048], P('expert', 'tensor'), may hold values from -0.21875 to 0.21875
Outputs:
- next_state: bfloat16 [8192, 2048], P('expert')
The draws below stay inside these ranges and needn't reach their ends.
Inputs may be any that keep to these rules, and one draw needn't show every extreme that they name: `expert_ids`: each row names 6 different experts. Within the rows of one index of the expert axis no expert is named by more than 512 rows, a bound that some block reaches.
All inputs are finite; a program needn't handle non-finite values.
Results may differ from the reference program's by a relative error of at most 0.009.
Values may be sent and summed in bfloat16 or wider, within the bound.
A program may use at most 192 MiB of HBM per device.

```python
import math
import jax
import jax.numpy as jnp
import numpy as np
from jax import lax

D = 2048
FF = 704
TOPK = 6
TOK_DEV = 1024
CAP = 512
EXPERTS = 16
TOKENS = 8192
N_EXPERT = 8
N_TENSOR = 4


def shard_levels(own_key, extent, shards, smallest, top_value):
    loudness, own = 1.0, jax.random.fold_in(own_key, 6)
    for position, shards_of in shards:
        draws = jnp.exp(jax.random.uniform(jax.random.fold_in(own, position), (shards_of,), jnp.float32, smallest / len(shards), top_value / len(shards)))
        loudness = loudness * jnp.repeat(draws, extent[position] // shards_of).reshape([-1 if axis == position else 1 for axis in range(len(extent))])
    return loudness


def shared_out(stream_key, own, number, rows, count, top, limit, skew):
    ranking = jax.random.permutation(stream_key, count)
    crowded, usual = shares(count, rows * top, limit, skew, True), shares(count, rows * top, limit, skew, False)
    places = jnp.arange(count)

    def named(tallies, offset_by):
        used = int((tallies > 0).sum())
        fixed = max(1, used // 4)
        moved = fixed + (places - fixed + offset_by * (used - fixed)) % max(1, count - fixed)
        return jnp.zeros((count,), jnp.int32).at[ranking[jnp.where(places < fixed, places, moved)]].set(jnp.asarray(tallies, jnp.int32))

    tallies = jnp.where(number % 4 == 0, named(crowded, number // 4), named(usual, number - number // 4 - 1))
    mixed = jax.random.permutation(jax.random.fold_in(own, 3), count)
    source_of, sink = mixed[0:count // 2 * 2:2], mixed[1:count // 2 * 2:2]
    slack = jnp.minimum(tallies[source_of] - 1, limit - tallies[sink]) // 2
    slack = jnp.where((source_of == ranking[0]) | (sink == ranking[0]) | (tallies[sink] == 0), 0, jnp.maximum(slack, 0))
    moved = jax.random.randint(jax.random.fold_in(own, 4), (count // 2,), 0, 1 << 20) % (slack + 1)
    tallies = tallies.at[source_of].add(-moved).at[sink].add(moved)
    labels = jnp.searchsorted(jnp.cumsum(tallies), jnp.arange(rows * top), side="right").astype(jnp.int32)
    grid = labels.reshape(top, rows).T
    grid = grid[jax.random.permutation(jax.random.fold_in(own, 1), rows)]
    offset_by = jax.random.randint(jax.random.fold_in(own, 2), (rows, 1), 0, top)
    return jnp.take_along_axis(grid, (jnp.arange(top)[None, :] + offset_by) % top, axis=1)


def shares(number_of, total, limit, lean, full):
    weights = [(1 << 20) // math.isqrt(grade ** lean) + 1 for grade in range(1, number_of + 1)]
    largest = limit if full else min(limit, max(-(-total // number_of), total * weights[0] // sum(weights)))
    least = 1 if total - largest >= number_of - 1 else 0
    counts, spare = [largest] + [least] * (number_of - 1), total - largest - least * (number_of - 1)
    while spare > 0:
        movable = [i for i in range(1, number_of) if counts[i] < largest] or [i for i in range(1, number_of) if counts[i] < limit]
        pool, left = sum([weights[i] for i in movable]), spare
        for i in movable:
            more = min(limit - counts[i], max(1, left * weights[i] // pool), spare)
            counts[i] = counts[i] + more
            spare = spare - more
    return np.array(counts)


def bell_draw(rng, shape, spread, limit, shards=(), kind=jnp.bfloat16):
    result = spread * jax.random.normal(rng, shape, jnp.float32)
    if shards:
        result = result * shard_levels(rng, shape, shards, -0.22, 0.18)
    return jnp.clip(result, -limit, limit).astype(kind)


def setup_inputs(seed: int = 0) -> dict:
    streams_of = jax.random.split(jax.random.key(seed), 8)
    flow_state = bell_draw(streams_of[0], (TOKENS, D), 1.0, 6.0, ((0, 8),))
    norm_gain = jnp.clip(1.0 + 0.1 * jax.random.normal(streams_of[1], (D,), jnp.float32), 0.5, 1.5)
    expert_ids_keys = jax.random.split(jax.random.fold_in(streams_of[2], 1), TOKENS // TOK_DEV)
    expert_ids_turns = jax.random.permutation(jax.random.fold_in(streams_of[2], 3), TOKENS // TOK_DEV)
    expert_ids = jax.vmap(lambda own, number: shared_out(jax.random.fold_in(streams_of[2], 2), own, number, TOK_DEV, EXPERTS, TOPK, CAP, 2))(expert_ids_keys, expert_ids_turns).reshape((TOKENS, TOPK))
    gate_weights = jnp.clip(0.1 + 0.9 * jax.random.uniform(streams_of[3], (TOKENS, TOPK), jnp.float32) ** shard_levels(streams_of[3], (TOKENS, TOPK), ((0, 8),), -0.2, 0.2), 0.1, 1.0)
    w_gate = bell_draw(streams_of[4], (EXPERTS, FF, D), D ** -0.5, 0.125, ((0, 8), (1, 4)))
    w_up = bell_draw(streams_of[5], (EXPERTS, FF, D), D ** -0.5, 0.125, ((0, 8), (1, 4)))
    w_down = bell_draw(streams_of[6], (EXPERTS, FF, D), FF ** -0.5, 0.21875, ((0, 8), (1, 4)))
    return {"flow_state": flow_state, "norm_gain": norm_gain, "expert_ids": expert_ids, "gate_weights": gate_weights, "w_gate": w_gate, "w_up": w_up, "w_down": w_down}


def reference(flow_state, norm_gain, expert_ids, gate_weights, w_gate, w_up, w_down):
    state_wide = flow_state.astype(jnp.float32)
    mean_square = lax.optimization_barrier(jnp.mean(state_wide * state_wide, axis=1, keepdims=True))
    normed = (state_wide * lax.rsqrt(mean_square + 1e-06) * norm_gain.astype(jnp.float32)[None, :]).astype(jnp.bfloat16)
    flat_ids = expert_ids.reshape(-1)
    flat_rows = (jnp.arange(flat_ids.shape[0], dtype=jnp.int32) // TOPK).astype(jnp.int32)
    flat_weights = gate_weights.reshape(-1).astype(jnp.float32)
    slot_span = N_EXPERT * CAP

    def tables(expert):
        matched = flat_ids == expert
        slot_ids = jnp.cumsum(matched.astype(jnp.int32)) - 1
        target = jnp.where(matched, slot_ids, slot_span).astype(jnp.int32)
        row_table = jnp.zeros((slot_span,), jnp.int32).at[target].set(flat_rows, mode='drop')
        weight_table = jnp.zeros((slot_span,), jnp.float32).at[target].set(flat_weights, mode='drop')
        return (row_table, weight_table)
    row_tables, weight_tables = lax.map(tables, jnp.arange(EXPERTS, dtype=jnp.int32))
    slices = FF // N_TENSOR
    summed = jnp.zeros((TOKENS, D), jnp.float32)
    for slice_index in range(N_TENSOR):
        low = slice_index * slices
        gate_slice = w_gate[:, low:low + slices, :]
        up_slice = w_up[:, low:low + slices, :]
        down_slice = w_down[:, low:low + slices, :]

        def expert_step(totals, carried):
            row_ids, row_weights, gate_block, up_block, down_block = carried
            picked = jnp.take(normed, row_ids, axis=0)
            gate_out = lax.dot_general(picked, gate_block, (((1,), (1,)), ((), ())), preferred_element_type=jnp.float32)
            up_out = lax.dot_general(picked, up_block, (((1,), (1,)), ((), ())), preferred_element_type=jnp.float32)
            activated = (jax.nn.silu(gate_out) * up_out).astype(jnp.bfloat16)
            output = jnp.dot(activated, down_block, preferred_element_type=jnp.float32)
            rounded_out = lax.optimization_barrier(output.astype(jnp.bfloat16))
            return (totals.at[row_ids].add(rounded_out.astype(jnp.float32) * row_weights[:, None]), None)
        partial_sum, _ = lax.scan(expert_step, jnp.zeros((TOKENS, D), jnp.float32), (row_tables, weight_tables, gate_slice, up_slice, down_slice))
        rounded = lax.optimization_barrier(partial_sum.astype(jnp.bfloat16))
        summed = summed + rounded.astype(jnp.float32)
    return (state_wide + summed).astype(jnp.bfloat16)
```

```python
import functools

import jax
import jax.numpy as jnp
from jax import lax
from jax.experimental import pallas as pl
from jax.experimental.pallas import tpu as pltpu
from jax.sharding import PartitionSpec as P

MESH = pl.DeviceIdType.MESH
CHUNKS = 4
ROW_TILE = 256


def kernel(
    groups,
    state_hbm,
    gain_ref,
    ids_ref,
    gw_ref,
    wg_hbm,
    wu_hbm,
    wd_hbm,
    out_hbm,
    gbuf,
    ubuf,
    dbuf,
    part,
    nrm,
    act,
    recv_sem,
    send_sem,
    local_sem,
    state_sem,
    out_sem,
):
    rows, width = nrm.shape
    exp_local, hidden, _ = wg_hbm.shape
    experts = gbuf.shape[0]
    ny = groups // 4
    half = width // 2
    col = width // CHUNKS
    me = lax.axis_index("expert")
    my_c = lax.rem(me, 2)
    my_x = lax.rem(me // 2, 2)
    my_y = me // 4

    def device(j, flip_x, flip_c):
        y = lax.rem(my_y + j, ny)
        x = 1 - my_x if flip_x else my_x
        c = 1 - my_c if flip_c else my_c
        return (y * 2 + x) * 2 + c

    x_peer = device(0, True, False)
    y_peers = [device(j, False, False) for j in range(1, ny)]
    sibling = device(0, False, True)

    pieces = []
    items = []
    for l in range(exp_local):
        p_half, q_half = [], []
        for src, buf in ((wg_hbm, gbuf), (wu_hbm, ubuf)):
            p_half.append(len(pieces))
            pieces.append((l, src, buf, 0, half))
            q_half.append(len(pieces))
            pieces.append((l, src, buf, half, half))
        items.append((p_half, q_half))
    for k in range(CHUNKS):
        p_half, q_half = [], []
        for l in range(exp_local):
            (p_half if l % 2 == 0 else q_half).append(len(pieces))
            pieces.append((l, wd_hbm, dbuf, k * col, col))
        items.append((p_half, q_half))

    def held(piece, source):
        l, _, buf, start, size = pieces[piece]
        return buf.at[source * exp_local + l, :, pl.ds(start, size)]

    def own(piece):
        l, src, _, start, size = pieces[piece]
        return src.at[l, :, pl.ds(start, size)]

    sent = []

    def send(piece, source, target, kind, is_own=False):
        copy = pltpu.make_async_remote_copy(
            src_ref=own(piece) if is_own else held(piece, source),
            dst_ref=held(piece, source),
            send_sem=send_sem.at[kind, piece, source],
            recv_sem=recv_sem.at[piece, source],
            device_id={"expert": target},
            device_id_type=MESH,
        )
        copy.start()
        sent.append(copy)

    def arrived(piece, source):
        pltpu.make_async_remote_copy(
            src_ref=held(piece, source),
            dst_ref=held(piece, source),
            send_sem=send_sem.at[0, piece, source],
            recv_sem=recv_sem.at[piece, source],
            device_id={"expert": sibling},
            device_id_type=MESH,
        ).wait_recv()

    def to_x(piece, source, is_own=False):
        send(piece, source, x_peer, 0, is_own)

    def to_core(piece, source, is_own=False):
        send(piece, source, sibling, 1, is_own)

    def to_y(piece, source, is_own=False):
        for n, peer in enumerate(y_peers):
            send(piece, source, peer, 2 + n, is_own)

    def start_own(item):
        p_half, q_half = items[item]
        for p, q in zip(p_half, q_half):
            to_x(p, me, True)
            to_y(q, me, True)
        for p, q in zip(p_half, q_half):
            to_x(q, me, True)
            to_y(p, me, True)
        for p, q in zip(p_half, q_half):
            to_core(p, me, True)
            to_core(q, me, True)

    def forward(item):
        p_half, q_half = items[item]
        for p, q in zip(p_half, q_half):
            arrived(p, x_peer)
            to_y(p, x_peer)
            to_core(p, x_peer)
            for peer in y_peers:
                arrived(q, peer)
                to_x(q, peer)
                to_core(q, peer)

    def second(item):
        p_half, q_half = items[item]
        for p, q in zip(p_half, q_half):
            arrived(q, x_peer)
            to_core(q, x_peer)
            for peer in y_peers:
                arrived(p, peer)
                to_core(p, peer)

    corners = [device(j, True, False) for j in range(1, ny)]

    def third(item):
        p_half, q_half = items[item]
        for p, q in zip(p_half, q_half):
            for corner in corners:
                arrived(p, corner)
                to_core(p, corner)
                arrived(q, corner)
                to_core(q, corner)

    def from_core(item, sources):
        p_half, q_half = items[item]
        for source in sources:
            for piece in p_half + q_half:
                arrived(piece, source)

    sib_x = device(0, True, True)
    sib_y = [device(j, False, True) for j in range(1, ny)]
    sib_corners = [device(j, True, True) for j in range(1, ny)]

    barrier = pltpu.get_barrier_semaphore()
    peers = [x_peer, sibling] + y_peers
    for peer in peers:
        pl.semaphore_signal(barrier, inc=1, device_id={"expert": peer}, device_id_type=MESH)
    pl.semaphore_wait(barrier, len(peers))

    start_own(0)
    load_state = pltpu.make_async_copy(state_hbm, part, state_sem)
    load_state.start()
    loads = []
    for n, (src, buf) in enumerate(((wg_hbm, gbuf), (wu_hbm, ubuf), (wd_hbm, dbuf))):
        copy = pltpu.make_async_copy(src, buf.at[pl.ds(me * exp_local, exp_local)], local_sem.at[n])
        copy.start()
        loads.append(copy)
    load_state.wait()

    @pl.loop(0, rows // 64)
    def _(i):
        span = pl.ds(pl.multiple_of(i * 64, 64), 64)
        wide = part[span, :].astype(jnp.float32)
        mean_square = jnp.mean(wide * wide, axis=1, keepdims=True)
        nrm[span, :] = (wide * lax.rsqrt(mean_square + 1e-06) * gain_ref[...]).astype(jnp.bfloat16)

    for copy in loads:
        copy.wait()

    def hidden_units(source, l):
        expert = source * exp_local + l

        @pl.loop(0, rows // ROW_TILE)
        def _(i):
            span = pl.ds(pl.multiple_of(i * ROW_TILE, ROW_TILE), ROW_TILE)
            a = nrm[span, :]
            dims = (((1,), (1,)), ((), ()))
            g = lax.dot_general(a, gbuf[expert], dims, preferred_element_type=jnp.float32)
            u = lax.dot_general(a, ubuf[expert], dims, preferred_element_type=jnp.float32)
            scale = jnp.sum(
                jnp.where(ids_ref[span, :] == expert, gw_ref[span, :], 0.0), axis=1, keepdims=True
            )
            act[expert, span, :] = (g / (1.0 + jnp.exp(-g)) * u * scale).astype(jnp.bfloat16)

    outs = []

    def outputs(k):
        @pl.loop(0, rows // ROW_TILE)
        def _(i):
            span = pl.ds(pl.multiple_of(i * ROW_TILE, ROW_TILE), ROW_TILE)
            total = jnp.zeros((ROW_TILE, col), jnp.float32)
            for expert in range(experts):
                total = total + jnp.dot(
                    act[expert, span, :],
                    dbuf[expert, :, k * col : (k + 1) * col],
                    preferred_element_type=jnp.float32,
                )
            part[span, k * col : (k + 1) * col] = total.astype(jnp.bfloat16)

        cols = pl.ds(k * col, col)
        copy = pltpu.make_async_copy(part.at[:, cols], out_hbm.at[:, cols], out_sem.at[k])
        copy.start()
        outs.append(copy)

    last = len(items) - 1
    for item in range(len(items)):
        forward(item)
        if item < last:
            start_own(item + 1)
        if item < exp_local:
            hidden_units(me, item)
            from_core(item, [sibling])
            hidden_units(sibling, item)
            second(item)
            for source in [x_peer] + y_peers:
                hidden_units(source, item)
            for source in [sib_x] + sib_y:
                from_core(item, [source])
                hidden_units(source, item)
            third(item)
            for source in corners:
                hidden_units(source, item)
            for source in sib_corners:
                from_core(item, [source])
                hidden_units(source, item)
        else:
            second(item)
            third(item)
            from_core(item, [sibling, sib_x] + sib_y + sib_corners)
            outputs(item - exp_local)
    for copy in sent:
        copy.wait_send()
    for copy in outs:
        copy.wait()


def shards(flow_state, norm_gain, expert_ids, gate_weights, w_gate, w_up, w_down):
    rows, width = flow_state.shape
    exp_local, hidden, _ = w_gate.shape
    groups = lax.axis_size("expert")
    experts = exp_local * groups
    n_pieces = exp_local * (4 + CHUNKS)
    weights = pltpu.VMEM((experts, hidden, width), jnp.bfloat16)
    any_space = pl.BlockSpec(memory_space=pl.ANY)
    vmem = pl.BlockSpec(memory_space=pltpu.VMEM)
    partial = pl.pallas_call(
        functools.partial(kernel, groups),
        out_shape=jax.ShapeDtypeStruct((rows, width), jnp.bfloat16),
        in_specs=[any_space, vmem, vmem, vmem, any_space, any_space, any_space],
        out_specs=any_space,
        scratch_shapes=[
            weights,
            weights,
            weights,
            pltpu.VMEM((rows, width), jnp.bfloat16),
            pltpu.VMEM((rows, width), jnp.bfloat16),
            pltpu.VMEM((experts, rows, hidden), jnp.bfloat16),
            pltpu.SemaphoreType.DMA((n_pieces, groups)),
            pltpu.SemaphoreType.DMA((groups // 4 + 1, n_pieces, groups)),
            pltpu.SemaphoreType.DMA((3,)),
            pltpu.SemaphoreType.DMA,
            pltpu.SemaphoreType.DMA((CHUNKS,)),
        ],
        compiler_params=pltpu.CompilerParams(
            collective_id=0, has_side_effects=True, vmem_limit_bytes=66 * 1000 * 1000
        ),
    )(
        flow_state,
        norm_gain.reshape(1, width),
        expert_ids,
        gate_weights,
        w_gate,
        w_up,
        w_down,
    )
    summed = lax.psum(partial, "tensor").astype(jnp.float32)
    return (flow_state.astype(jnp.float32) + summed).astype(jnp.bfloat16)


def solution(mesh):
    return jax.shard_map(
        shards,
        mesh=mesh,
        in_specs=(
            P("expert", None),
            P(),
            P("expert", None),
            P("expert", None),
            P("expert", "tensor", None),
            P("expert", "tensor", None),
            P("expert", "tensor", None),
        ),
        out_specs=P("expert", None),
        check_vma=False,
    )
```

```python
import functools

import jax
import jax.numpy as jnp
from jax import lax
from jax.experimental import pallas as pl
from jax.experimental.pallas import tpu as pltpu
from jax.sharding import PartitionSpec as P

MESH = pl.DeviceIdType.MESH
CHUNKS = 4
ROW_TILE = 256


def kernel(
    groups,
    slices,
    state_hbm,
    gain_ref,
    ids_ref,
    gw_ref,
    wg_hbm,
    wu_hbm,
    wd_hbm,
    out_hbm,
    gbuf,
    ubuf,
    dbuf,
    part,
    nrm,
    act,
    zin,
    own_state,
    recv_sem,
    send_sem,
    local_sem,
    state_sem,
    out_sem,
    rs_recv,
    rs_send,
    fin_send,
    ag_recv,
    ag_send,
):
    rows, width = nrm.shape
    exp_local, hidden, _ = wg_hbm.shape
    experts = gbuf.shape[0]
    ny = groups // 4
    half = width // 2
    col = width // CHUNKS
    z_rows = rows // slices
    z_tile = min(z_rows, 64)
    me = lax.axis_index("expert")
    my_c = lax.rem(me, 2)
    my_x = lax.rem(me // 2, 2)
    my_y = me // 4

    def device(j, flip_x, flip_c):
        y = lax.rem(my_y + j, ny)
        x = 1 - my_x if flip_x else my_x
        c = 1 - my_c if flip_c else my_c
        return (y * 2 + x) * 2 + c

    x_peer = device(0, True, False)
    y_peers = [device(j, False, False) for j in range(1, ny)]
    sibling = device(0, False, True)

    pieces = []
    items = []
    for l in range(exp_local):
        p_half, q_half = [], []
        for src, buf in ((wg_hbm, gbuf), (wu_hbm, ubuf)):
            p_half.append(len(pieces))
            pieces.append((l, src, buf, 0, half))
            q_half.append(len(pieces))
            pieces.append((l, src, buf, half, half))
        items.append((p_half, q_half))
    for k in range(CHUNKS):
        p_half, q_half = [], []
        for l in range(exp_local):
            (p_half if l % 2 == 0 else q_half).append(len(pieces))
            pieces.append((l, wd_hbm, dbuf, k * col, col))
        items.append((p_half, q_half))

    def held(piece, source):
        l, _, buf, start, size = pieces[piece]
        return buf.at[source * exp_local + l, :, pl.ds(start, size)]

    def own(piece):
        l, src, _, start, size = pieces[piece]
        return src.at[l, :, pl.ds(start, size)]

    sent = []

    def send(piece, source, target, kind, is_own=False):
        copy = pltpu.make_async_remote_copy(
            src_ref=own(piece) if is_own else held(piece, source),
            dst_ref=held(piece, source),
            send_sem=send_sem.at[kind, piece, source],
            recv_sem=recv_sem.at[piece, source],
            device_id={"expert": target},
            device_id_type=MESH,
        )
        copy.start()
        sent.append(copy)

    def arrived(piece, source):
        pltpu.make_async_remote_copy(
            src_ref=held(piece, source),
            dst_ref=held(piece, source),
            send_sem=send_sem.at[0, piece, source],
            recv_sem=recv_sem.at[piece, source],
            device_id={"expert": sibling},
            device_id_type=MESH,
        ).wait_recv()

    def to_x(piece, source, is_own=False):
        send(piece, source, x_peer, 0, is_own)

    def to_core(piece, source, is_own=False):
        send(piece, source, sibling, 1, is_own)

    def to_y(piece, source, is_own=False):
        for n, peer in enumerate(y_peers):
            send(piece, source, peer, 2 + n, is_own)

    def start_own(item):
        p_half, q_half = items[item]
        for p, q in zip(p_half, q_half):
            to_x(p, me, True)
            to_y(q, me, True)
        for p, q in zip(p_half, q_half):
            to_x(q, me, True)
            to_y(p, me, True)
        for p, q in zip(p_half, q_half):
            to_core(p, me, True)
            to_core(q, me, True)

    def forward(item):
        p_half, q_half = items[item]
        for p, q in zip(p_half, q_half):
            arrived(p, x_peer)
            to_y(p, x_peer)
            to_core(p, x_peer)
            for peer in y_peers:
                arrived(q, peer)
                to_x(q, peer)
                to_core(q, peer)

    def second(item):
        p_half, q_half = items[item]
        for p, q in zip(p_half, q_half):
            arrived(q, x_peer)
            to_core(q, x_peer)
            for peer in y_peers:
                arrived(p, peer)
                to_core(p, peer)

    corners = [device(j, True, False) for j in range(1, ny)]

    def third(item):
        p_half, q_half = items[item]
        for p, q in zip(p_half, q_half):
            for corner in corners:
                arrived(p, corner)
                to_core(p, corner)
                arrived(q, corner)
                to_core(q, corner)

    def from_core(item, sources):
        p_half, q_half = items[item]
        for source in sources:
            for piece in p_half + q_half:
                arrived(piece, source)

    sib_x = device(0, True, True)
    sib_y = [device(j, False, True) for j in range(1, ny)]
    sib_corners = [device(j, True, True) for j in range(1, ny)]

    at = lax.axis_index("tensor")
    right, left = lax.rem(at + 1, slices), lax.rem(at + slices - 1, slices)
    barrier = pltpu.get_barrier_semaphore()
    peers = [{"expert": peer} for peer in [x_peer, sibling] + y_peers]
    peers += [{"tensor": right}, {"tensor": left}]
    for peer in peers:
        pl.semaphore_signal(barrier, inc=1, device_id=peer, device_id_type=MESH)
    pl.semaphore_wait(barrier, len(peers))

    start_own(0)
    load_state = pltpu.make_async_copy(state_hbm, part, state_sem)
    load_state.start()
    loads = []
    for n, (src, buf) in enumerate(((wg_hbm, gbuf), (wu_hbm, ubuf), (wd_hbm, dbuf))):
        copy = pltpu.make_async_copy(src, buf.at[pl.ds(me * exp_local, exp_local)], local_sem.at[n])
        copy.start()
        loads.append(copy)
    load_own = pltpu.make_async_copy(
        state_hbm.at[pl.ds(at * z_rows, z_rows)], own_state, local_sem.at[3]
    )
    load_own.start()
    loads.append(load_own)
    load_state.wait()

    @pl.loop(0, rows // 64)
    def _(i):
        span = pl.ds(pl.multiple_of(i * 64, 64), 64)
        wide = part[span, :].astype(jnp.float32)
        mean_square = jnp.mean(wide * wide, axis=1, keepdims=True)
        nrm[span, :] = (wide * lax.rsqrt(mean_square + 1e-06) * gain_ref[...]).astype(jnp.bfloat16)

    for copy in loads:
        copy.wait()

    def hidden_units(source, l):
        expert = source * exp_local + l

        @pl.loop(0, rows // ROW_TILE)
        def _(i):
            span = pl.ds(pl.multiple_of(i * ROW_TILE, ROW_TILE), ROW_TILE)
            a = nrm[span, :]
            dims = (((1,), (1,)), ((), ()))
            g = lax.dot_general(a, gbuf[expert], dims, preferred_element_type=jnp.float32)
            u = lax.dot_general(a, ubuf[expert], dims, preferred_element_type=jnp.float32)
            scale = jnp.sum(
                jnp.where(ids_ref[span, :] == expert, gw_ref[span, :], 0.0), axis=1, keepdims=True
            )
            act[expert, span, :] = (g / (1.0 + jnp.exp(-g)) * u * scale).astype(jnp.bfloat16)

    def outputs(k):
        @pl.loop(0, rows // ROW_TILE)
        def _(i):
            span = pl.ds(pl.multiple_of(i * ROW_TILE, ROW_TILE), ROW_TILE)
            total = jnp.zeros((ROW_TILE, col), jnp.float32)
            for expert in range(experts):
                total = total + jnp.dot(
                    act[expert, span, :],
                    dbuf[expert, :, k * col : (k + 1) * col],
                    preferred_element_type=jnp.float32,
                )
            part[span, k * col : (k + 1) * col] = total.astype(jnp.bfloat16)

    def block(ref, k, q):
        return ref.at[pl.ds(pl.multiple_of(q * z_rows, z_rows), z_rows), pl.ds(k * col, col)]

    def sum_copy(k, q, slot, target):
        return pltpu.make_async_remote_copy(
            src_ref=block(part, k, q),
            dst_ref=zin.at[k, slot],
            send_sem=rs_send.at[k, q],
            recv_sem=rs_recv.at[k, slot],
            device_id={"tensor": target},
            device_id_type=MESH,
        )

    def final_copy(k, q, source, sem, target):
        return pltpu.make_async_remote_copy(
            src_ref=block(source, k, q),
            dst_ref=block(out_hbm, k, q),
            send_sem=sem,
            recv_sem=ag_recv.at[k, q],
            device_id={"tensor": target},
            device_id_type=MESH,
        )

    def local_copy(k):
        return pltpu.make_async_copy(block(part, k, at), block(out_hbm, k, at), out_sem.at[k])

    def add_in(k, q, slot):
        sum_copy(k, q, slot, right).wait_recv()

        @pl.loop(0, z_rows // z_tile)
        def _(i):
            inner = pl.ds(pl.multiple_of(i * z_tile, z_tile), z_tile)
            span = pl.ds(pl.multiple_of(q * z_rows + i * z_tile, z_tile), z_tile)
            total = part[span, k * col : (k + 1) * col].astype(jnp.float32)
            total = total + zin[k, slot, inner, :].astype(jnp.float32)
            part[span, k * col : (k + 1) * col] = total.astype(jnp.bfloat16)

    def sums(k, d):
        @pl.when(at + d < slices)
        def _():
            @pl.when(at > 0)
            def _():
                add_in(k, at + d, at + d)

            sum_copy(k, at + d, at + d, right).start()

        @pl.when(at - d >= 0)
        def _():
            @pl.when(at < slices - 1)
            def _():
                add_in(k, at - d, at - d)

            sum_copy(k, at - d, slices if d == 1 else at - d, left).start()

    def finish(k):
        cols = slice(k * col, (k + 1) * col)

        def rounds(slots):
            for slot in slots:
                sum_copy(k, at, slot, right).wait_recv()

            @pl.loop(0, z_rows // z_tile)
            def _(i):
                inner = pl.ds(pl.multiple_of(i * z_tile, z_tile), z_tile)
                span = pl.ds(pl.multiple_of(at * z_rows + i * z_tile, z_tile), z_tile)
                total = part[span, cols].astype(jnp.float32)
                for slot in slots:
                    total = total + zin[k, slot, inner, :].astype(jnp.float32)
                total = total + own_state[inner, cols].astype(jnp.float32)
                part[span, cols] = total.astype(jnp.bfloat16)

        @pl.when(at == 0)
        def _():
            rounds([slices])

        @pl.when(at == slices - 1)
        def _():
            rounds([at])

        @pl.when((at > 0) & (at < slices - 1))
        def _():
            rounds([at, slices])

        @pl.when(at < slices - 1)
        def _():
            final_copy(k, at, part, fin_send.at[k, 0], right).start()

        @pl.when(at > 0)
        def _():
            final_copy(k, at, part, fin_send.at[k, 1], left).start()

        local_copy(k).start()

    def passes(k, d):
        @pl.when(at - d >= 0)
        def _():
            final_copy(k, at - d, out_hbm, ag_send.at[k, at - d], right).wait_recv()

            @pl.when(at < slices - 1)
            def _():
                final_copy(k, at - d, out_hbm, ag_send.at[k, at - d], right).start()

        @pl.when(at + d < slices)
        def _():
            final_copy(k, at + d, out_hbm, ag_send.at[k, at + d], left).wait_recv()

            @pl.when(at > 0)
            def _():
                final_copy(k, at + d, out_hbm, ag_send.at[k, at + d], left).start()

    def drain(k):
        for d in range(1, slices):

            @pl.when(at + d < slices)
            def _():
                sum_copy(k, at + d, at + d, right).wait_send()

                @pl.when(at > 0)
                def _():
                    final_copy(k, at + d, out_hbm, ag_send.at[k, at + d], left).wait_send()

            @pl.when(at - d >= 0)
            def _():
                sum_copy(k, at - d, at - d, left).wait_send()

                @pl.when(at < slices - 1)
                def _():
                    final_copy(k, at - d, out_hbm, ag_send.at[k, at - d], right).wait_send()

        @pl.when(at < slices - 1)
        def _():
            final_copy(k, at, part, fin_send.at[k, 0], right).wait_send()

        @pl.when(at > 0)
        def _():
            final_copy(k, at, part, fin_send.at[k, 1], left).wait_send()

        local_copy(k).wait()

    def chain(k, stage):
        if not 0 <= k < CHUNKS:
            return
        if stage == "first":
            sums(k, slices - 1)
        elif stage == "middle":
            for d in range(slices - 2, 1, -1):
                sums(k, d)
        elif stage == "last":
            if slices > 2:
                sums(k, 1)
        elif stage == "finish":
            finish(k)
        elif stage == "near":
            passes(k, 1)
        elif stage == "far":
            for d in range(2, slices - 1):
                passes(k, d)
        elif stage == "farthest":
            if slices > 2:
                passes(k, slices - 1)

    last = len(items) - 1
    for item in range(len(items)):
        k = item - exp_local
        forward(item)
        if item < last:
            start_own(item + 1)
        if item < exp_local:
            hidden_units(me, item)
            from_core(item, [sibling])
            hidden_units(sibling, item)
            second(item)
            for source in [x_peer] + y_peers:
                hidden_units(source, item)
            for source in [sib_x] + sib_y:
                from_core(item, [source])
                hidden_units(source, item)
            third(item)
            for source in corners:
                hidden_units(source, item)
            for source in sib_corners:
                from_core(item, [source])
                hidden_units(source, item)
        else:
            chain(k - 1, "middle")
            chain(k - 2, "far")
            second(item)
            chain(k - 1, "last")
            chain(k - 2, "farthest")
            third(item)
            from_core(item, [sibling, sib_x] + sib_y + sib_corners)
            chain(k - 1, "finish")
            outputs(k)
            chain(k, "first")
            chain(k - 1, "near")
    end = CHUNKS - 1
    chain(end, "middle")
    chain(end - 1, "far")
    chain(end, "last")
    chain(end - 1, "farthest")
    for stage in ("finish", "near", "far", "farthest"):
        chain(end, stage)
    for copy in sent:
        copy.wait_send()
    for k in range(CHUNKS):
        drain(k)


def shards(flow_state, norm_gain, expert_ids, gate_weights, w_gate, w_up, w_down):
    rows, width = flow_state.shape
    exp_local, hidden, _ = w_gate.shape
    groups = lax.axis_size("expert")
    slices = lax.axis_size("tensor")
    experts = exp_local * groups
    n_pieces = exp_local * (4 + CHUNKS)
    weights = pltpu.VMEM((experts, hidden, width), jnp.bfloat16)
    any_space = pl.BlockSpec(memory_space=pl.ANY)
    vmem = pl.BlockSpec(memory_space=pltpu.VMEM)
    return pl.pallas_call(
        functools.partial(kernel, groups, slices),
        out_shape=jax.ShapeDtypeStruct((rows, width), jnp.bfloat16),
        in_specs=[any_space, vmem, vmem, vmem, any_space, any_space, any_space],
        out_specs=any_space,
        scratch_shapes=[
            weights,
            weights,
            weights,
            pltpu.VMEM((rows, width), jnp.bfloat16),
            pltpu.VMEM((rows, width), jnp.bfloat16),
            pltpu.VMEM((experts, rows, hidden), jnp.bfloat16),
            pltpu.VMEM((CHUNKS, slices + 1, rows // slices, width // CHUNKS), jnp.bfloat16),
            pltpu.VMEM((rows // slices, width), jnp.bfloat16),
            pltpu.SemaphoreType.DMA((n_pieces, groups)),
            pltpu.SemaphoreType.DMA((groups // 4 + 1, n_pieces, groups)),
            pltpu.SemaphoreType.DMA((4,)),
            pltpu.SemaphoreType.DMA,
            pltpu.SemaphoreType.DMA((CHUNKS,)),
            pltpu.SemaphoreType.DMA((CHUNKS, slices + 1)),
            pltpu.SemaphoreType.DMA((CHUNKS, slices)),
            pltpu.SemaphoreType.DMA((CHUNKS, 2)),
            pltpu.SemaphoreType.DMA((CHUNKS, slices)),
            pltpu.SemaphoreType.DMA((CHUNKS, slices)),
        ],
        compiler_params=pltpu.CompilerParams(
            collective_id=0, has_side_effects=True, vmem_limit_bytes=66 * 1000 * 1000
        ),
    )(
        flow_state,
        norm_gain.reshape(1, width),
        expert_ids,
        gate_weights,
        w_gate,
        w_up,
        w_down,
    )


def solution(mesh):
    return jax.shard_map(
        shards,
        mesh=mesh,
        in_specs=(
            P("expert", None),
            P(),
            P("expert", None),
            P("expert", None),
            P("expert", "tensor", None),
            P("expert", "tensor", None),
            P("expert", "tensor", None),
        ),
        out_specs=P("expert", None),
        check_vma=False,
    )
```

```python
import functools

import jax
import jax.numpy as jnp
from jax import lax
from jax.experimental import pallas as pl
from jax.experimental.pallas import tpu as pltpu
from jax.sharding import PartitionSpec as P

MESH = pl.DeviceIdType.MESH
CHUNKS = 8
ROW_TILE = 256


def kernel(
    groups,
    slices,
    state_hbm,
    gain_ref,
    ids_ref,
    gw_ref,
    wg_hbm,
    wu_hbm,
    wd_hbm,
    out_hbm,
    gbuf,
    ubuf,
    dbuf,
    part,
    nrm,
    act,
    zin,
    own_state,
    recv_sem,
    send_sem,
    local_sem,
    state_sem,
    out_sem,
    rs_recv,
    rs_send,
    fin_send,
    ag_recv,
    ag_send,
):
    rows, width = nrm.shape
    exp_local, hidden, _ = wg_hbm.shape
    experts = gbuf.shape[0]
    ny = groups // 4
    half = width // 2
    col = width // CHUNKS
    z_rows = rows // slices
    z_tile = min(z_rows, 64)
    me = lax.axis_index("expert")
    my_c = lax.rem(me, 2)
    my_x = lax.rem(me // 2, 2)
    my_y = me // 4

    def device(j, flip_x, flip_c):
        y = lax.rem(my_y + j, ny)
        x = 1 - my_x if flip_x else my_x
        c = 1 - my_c if flip_c else my_c
        return (y * 2 + x) * 2 + c

    x_peer = device(0, True, False)
    y_peers = [device(j, False, False) for j in range(1, ny)]
    sibling = device(0, False, True)

    pieces = []
    items = []
    for l in range(exp_local):
        p_half, q_half = [], []
        for src, buf in ((wg_hbm, gbuf), (wu_hbm, ubuf)):
            p_half.append(len(pieces))
            pieces.append((l, src, buf, 0, half))
            q_half.append(len(pieces))
            pieces.append((l, src, buf, half, half))
        items.append((p_half, q_half))
    for k in range(CHUNKS):
        p_half, q_half = [], []
        for l in range(exp_local):
            (p_half if l % 2 == 0 else q_half).append(len(pieces))
            pieces.append((l, wd_hbm, dbuf, k * col, col))
        items.append((p_half, q_half))

    def held(piece, source):
        l, _, buf, start, size = pieces[piece]
        return buf.at[source * exp_local + l, :, pl.ds(start, size)]

    def own(piece):
        l, src, _, start, size = pieces[piece]
        return src.at[l, :, pl.ds(start, size)]

    sent = []

    def send(piece, source, target, kind, is_own=False):
        copy = pltpu.make_async_remote_copy(
            src_ref=own(piece) if is_own else held(piece, source),
            dst_ref=held(piece, source),
            send_sem=send_sem.at[kind, piece, source],
            recv_sem=recv_sem.at[piece, source],
            device_id={"expert": target},
            device_id_type=MESH,
        )
        copy.start()
        sent.append(copy)

    def arrived(piece, source):
        pltpu.make_async_remote_copy(
            src_ref=held(piece, source),
            dst_ref=held(piece, source),
            send_sem=send_sem.at[0, piece, source],
            recv_sem=recv_sem.at[piece, source],
            device_id={"expert": sibling},
            device_id_type=MESH,
        ).wait_recv()

    def to_x(piece, source, is_own=False):
        send(piece, source, x_peer, 0, is_own)

    def to_core(piece, source, is_own=False):
        send(piece, source, sibling, 1, is_own)

    def to_y(piece, source, is_own=False):
        for n, peer in enumerate(y_peers):
            send(piece, source, peer, 2 + n, is_own)

    def start_own(item):
        p_half, q_half = items[item]
        for p, q in zip(p_half, q_half):
            to_x(p, me, True)
            to_y(q, me, True)
        for p, q in zip(p_half, q_half):
            to_x(q, me, True)
            to_y(p, me, True)
        for p, q in zip(p_half, q_half):
            to_core(p, me, True)
            to_core(q, me, True)

    def forward(item):
        p_half, q_half = items[item]
        for p, q in zip(p_half, q_half):
            arrived(p, x_peer)
            to_y(p, x_peer)
            to_core(p, x_peer)
            for peer in y_peers:
                arrived(q, peer)
                to_x(q, peer)
                to_core(q, peer)

    def second(item):
        p_half, q_half = items[item]
        for p, q in zip(p_half, q_half):
            arrived(q, x_peer)
            to_core(q, x_peer)
            for peer in y_peers:
                arrived(p, peer)
                to_core(p, peer)

    corners = [device(j, True, False) for j in range(1, ny)]

    def third(item):
        p_half, q_half = items[item]
        for p, q in zip(p_half, q_half):
            for corner in corners:
                arrived(p, corner)
                to_core(p, corner)
                arrived(q, corner)
                to_core(q, corner)

    def from_core(item, sources):
        p_half, q_half = items[item]
        for source in sources:
            for piece in p_half + q_half:
                arrived(piece, source)

    sib_x = device(0, True, True)
    sib_y = [device(j, False, True) for j in range(1, ny)]
    sib_corners = [device(j, True, True) for j in range(1, ny)]

    at = lax.axis_index("tensor")
    right, left = lax.rem(at + 1, slices), lax.rem(at + slices - 1, slices)
    barrier = pltpu.get_barrier_semaphore()
    peers = [{"expert": peer} for peer in [x_peer, sibling] + y_peers]
    peers += [{"tensor": right}, {"tensor": left}]
    for peer in peers:
        pl.semaphore_signal(barrier, inc=1, device_id=peer, device_id_type=MESH)
    pl.semaphore_wait(barrier, len(peers))

    start_own(0)
    load_state = pltpu.make_async_copy(state_hbm, part, state_sem)
    load_state.start()
    loads = []
    for n, (src, buf) in enumerate(((wg_hbm, gbuf), (wu_hbm, ubuf), (wd_hbm, dbuf))):
        copy = pltpu.make_async_copy(src, buf.at[pl.ds(me * exp_local, exp_local)], local_sem.at[n])
        copy.start()
        loads.append(copy)
    load_own = pltpu.make_async_copy(
        state_hbm.at[pl.ds(at * z_rows, z_rows)], own_state, local_sem.at[3]
    )
    load_own.start()
    loads.append(load_own)
    load_state.wait()

    @pl.loop(0, rows // 64)
    def _(i):
        span = pl.ds(pl.multiple_of(i * 64, 64), 64)
        wide = part[span, :].astype(jnp.float32)
        mean_square = jnp.mean(wide * wide, axis=1, keepdims=True)
        nrm[span, :] = (wide * lax.rsqrt(mean_square + 1e-06) * gain_ref[...]).astype(jnp.bfloat16)

    for copy in loads:
        copy.wait()

    def hidden_units(source, l):
        expert = source * exp_local + l

        @pl.loop(0, rows // ROW_TILE)
        def _(i):
            span = pl.ds(pl.multiple_of(i * ROW_TILE, ROW_TILE), ROW_TILE)
            a = nrm[span, :]
            dims = (((1,), (1,)), ((), ()))
            g = lax.dot_general(a, gbuf[expert], dims, preferred_element_type=jnp.float32)
            u = lax.dot_general(a, ubuf[expert], dims, preferred_element_type=jnp.float32)
            scale = jnp.sum(
                jnp.where(ids_ref[span, :] == expert, gw_ref[span, :], 0.0), axis=1, keepdims=True
            )
            act[expert, span, :] = (g / (1.0 + jnp.exp(-g)) * u * scale).astype(jnp.bfloat16)

    def outputs(k):
        @pl.loop(0, rows // ROW_TILE)
        def _(i):
            span = pl.ds(pl.multiple_of(i * ROW_TILE, ROW_TILE), ROW_TILE)
            total = jnp.zeros((ROW_TILE, col), jnp.float32)
            for expert in range(experts):
                total = total + jnp.dot(
                    act[expert, span, :],
                    dbuf[expert, :, k * col : (k + 1) * col],
                    preferred_element_type=jnp.float32,
                )
            part[span, k * col : (k + 1) * col] = total.astype(jnp.bfloat16)

    def block(ref, k, q):
        return ref.at[pl.ds(pl.multiple_of(q * z_rows, z_rows), z_rows), pl.ds(k * col, col)]

    def sum_copy(k, q, slot, target):
        return pltpu.make_async_remote_copy(
            src_ref=block(part, k, q),
            dst_ref=zin.at[k, slot],
            send_sem=rs_send.at[k, q],
            recv_sem=rs_recv.at[k, slot],
            device_id={"tensor": target},
            device_id_type=MESH,
        )

    def final_copy(k, q, source, sem, target):
        return pltpu.make_async_remote_copy(
            src_ref=block(source, k, q),
            dst_ref=block(out_hbm, k, q),
            send_sem=sem,
            recv_sem=ag_recv.at[k, q],
            device_id={"tensor": target},
            device_id_type=MESH,
        )

    def local_copy(k):
        return pltpu.make_async_copy(block(part, k, at), block(out_hbm, k, at), out_sem.at[k])

    def add_in(k, q, slot):
        sum_copy(k, q, slot, right).wait_recv()

        @pl.loop(0, z_rows // z_tile)
        def _(i):
            inner = pl.ds(pl.multiple_of(i * z_tile, z_tile), z_tile)
            span = pl.ds(pl.multiple_of(q * z_rows + i * z_tile, z_tile), z_tile)
            total = part[span, k * col : (k + 1) * col].astype(jnp.float32)
            total = total + zin[k, slot, inner, :].astype(jnp.float32)
            part[span, k * col : (k + 1) * col] = total.astype(jnp.bfloat16)

    def sums(k, d):
        @pl.when(at + d < slices)
        def _():
            @pl.when(at > 0)
            def _():
                add_in(k, at + d, at + d)

            sum_copy(k, at + d, at + d, right).start()

        @pl.when(at - d >= 0)
        def _():
            @pl.when(at < slices - 1)
            def _():
                add_in(k, at - d, at - d)

            sum_copy(k, at - d, slices if d == 1 else at - d, left).start()

    def finish(k):
        cols = slice(k * col, (k + 1) * col)

        def rounds(slots):
            for slot in slots:
                sum_copy(k, at, slot, right).wait_recv()

            @pl.loop(0, z_rows // z_tile)
            def _(i):
                inner = pl.ds(pl.multiple_of(i * z_tile, z_tile), z_tile)
                span = pl.ds(pl.multiple_of(at * z_rows + i * z_tile, z_tile), z_tile)
                total = part[span, cols].astype(jnp.float32)
                for slot in slots:
                    total = total + zin[k, slot, inner, :].astype(jnp.float32)
                total = total + own_state[inner, cols].astype(jnp.float32)
                part[span, cols] = total.astype(jnp.bfloat16)

        @pl.when(at == 0)
        def _():
            rounds([slices])

        @pl.when(at == slices - 1)
        def _():
            rounds([at])

        @pl.when((at > 0) & (at < slices - 1))
        def _():
            rounds([at, slices])

        @pl.when(at < slices - 1)
        def _():
            final_copy(k, at, part, fin_send.at[k, 0], right).start()

        @pl.when(at > 0)
        def _():
            final_copy(k, at, part, fin_send.at[k, 1], left).start()

        local_copy(k).start()

    def passes(k, d):
        @pl.when(at - d >= 0)
        def _():
            final_copy(k, at - d, out_hbm, ag_send.at[k, at - d], right).wait_recv()

            @pl.when(at < slices - 1)
            def _():
                final_copy(k, at - d, out_hbm, ag_send.at[k, at - d], right).start()

        @pl.when(at + d < slices)
        def _():
            final_copy(k, at + d, out_hbm, ag_send.at[k, at + d], left).wait_recv()

            @pl.when(at > 0)
            def _():
                final_copy(k, at + d, out_hbm, ag_send.at[k, at + d], left).start()

    def drain(k):
        for d in range(1, slices):

            @pl.when(at + d < slices)
            def _():
                sum_copy(k, at + d, at + d, right).wait_send()

                @pl.when(at > 0)
                def _():
                    final_copy(k, at + d, out_hbm, ag_send.at[k, at + d], left).wait_send()

            @pl.when(at - d >= 0)
            def _():
                sum_copy(k, at - d, at - d, left).wait_send()

                @pl.when(at < slices - 1)
                def _():
                    final_copy(k, at - d, out_hbm, ag_send.at[k, at - d], right).wait_send()

        @pl.when(at < slices - 1)
        def _():
            final_copy(k, at, part, fin_send.at[k, 0], right).wait_send()

        @pl.when(at > 0)
        def _():
            final_copy(k, at, part, fin_send.at[k, 1], left).wait_send()

        local_copy(k).wait()

    def chain(k, stage):
        if not 0 <= k < CHUNKS:
            return
        if stage == "first":
            sums(k, slices - 1)
        elif stage == "middle":
            for d in range(slices - 2, 1, -1):
                sums(k, d)
        elif stage == "last":
            if slices > 2:
                sums(k, 1)
        elif stage == "finish":
            finish(k)
        elif stage == "near":
            passes(k, 1)
        elif stage == "far":
            for d in range(2, slices - 1):
                passes(k, d)
        elif stage == "farthest":
            if slices > 2:
                passes(k, slices - 1)

    last = len(items) - 1
    for item in range(len(items)):
        k = item - exp_local
        forward(item)
        if item < last:
            start_own(item + 1)
        if item < exp_local:
            hidden_units(me, item)
            from_core(item, [sibling])
            hidden_units(sibling, item)
            second(item)
            for source in [x_peer] + y_peers:
                hidden_units(source, item)
            for source in [sib_x] + sib_y:
                from_core(item, [source])
                hidden_units(source, item)
            third(item)
            for source in corners:
                hidden_units(source, item)
            for source in sib_corners:
                from_core(item, [source])
                hidden_units(source, item)
        else:
            chain(k - 6, "farthest")
            chain(k - 5, "far")
            second(item)
            chain(k - 4, "near")
            chain(k - 3, "finish")
            third(item)
            chain(k - 2, "last")
            chain(k - 1, "middle")
            from_core(item, [sibling, sib_x] + sib_y + sib_corners)
            outputs(k)
            chain(k, "first")
    for k in range(CHUNKS, CHUNKS + 6):
        chain(k - 6, "farthest")
        chain(k - 5, "far")
        chain(k - 4, "near")
        chain(k - 3, "finish")
        chain(k - 2, "last")
        chain(k - 1, "middle")
    for copy in sent:
        copy.wait_send()
    for k in range(CHUNKS):
        drain(k)


def shards(flow_state, norm_gain, expert_ids, gate_weights, w_gate, w_up, w_down):
    rows, width = flow_state.shape
    exp_local, hidden, _ = w_gate.shape
    groups = lax.axis_size("expert")
    slices = lax.axis_size("tensor")
    experts = exp_local * groups
    n_pieces = exp_local * (4 + CHUNKS)
    weights = pltpu.VMEM((experts, hidden, width), jnp.bfloat16)
    any_space = pl.BlockSpec(memory_space=pl.ANY)
    vmem = pl.BlockSpec(memory_space=pltpu.VMEM)
    return pl.pallas_call(
        functools.partial(kernel, groups, slices),
        out_shape=jax.ShapeDtypeStruct((rows, width), jnp.bfloat16),
        in_specs=[any_space, vmem, vmem, vmem, any_space, any_space, any_space],
        out_specs=any_space,
        scratch_shapes=[
            weights,
            weights,
            weights,
            pltpu.VMEM((rows, width), jnp.bfloat16),
            pltpu.VMEM((rows, width), jnp.bfloat16),
            pltpu.VMEM((experts, rows, hidden), jnp.bfloat16),
            pltpu.VMEM((CHUNKS, slices + 1, rows // slices, width // CHUNKS), jnp.bfloat16),
            pltpu.VMEM((rows // slices, width), jnp.bfloat16),
            pltpu.SemaphoreType.DMA((n_pieces, groups)),
            pltpu.SemaphoreType.DMA((groups // 4 + 1, n_pieces, groups)),
            pltpu.SemaphoreType.DMA((4,)),
            pltpu.SemaphoreType.DMA,
            pltpu.SemaphoreType.DMA((CHUNKS,)),
            pltpu.SemaphoreType.DMA((CHUNKS, slices + 1)),
            pltpu.SemaphoreType.DMA((CHUNKS, slices)),
            pltpu.SemaphoreType.DMA((CHUNKS, 2)),
            pltpu.SemaphoreType.DMA((CHUNKS, slices)),
            pltpu.SemaphoreType.DMA((CHUNKS, slices)),
        ],
        compiler_params=pltpu.CompilerParams(
            collective_id=0, has_side_effects=True, vmem_limit_bytes=66 * 1000 * 1000
        ),
    )(
        flow_state,
        norm_gain.reshape(1, width),
        expert_ids,
        gate_weights,
        w_gate,
        w_up,
        w_down,
    )


def solution(mesh):
    return jax.shard_map(
        shards,
        mesh=mesh,
        in_specs=(
            P("expert", None),
            P(),
            P("expert", None),
            P("expert", None),
            P("expert", "tensor", None),
            P("expert", "tensor", None),
            P("expert", "tensor", None),
        ),
        out_specs=P("expert", None),
        check_vma=False,
    )
```
